1024 devices in a mesh: grid: 64 (over y, x), day: 16 (over z, core).
Axes of the slice: x: 8, y: 8, z: 8, core: 2. Of those that a mesh axis runs over, the one named last changes fastest.
Arguments:
- fields: bfloat16 [6144, 262144], P('day', 'grid')
- eof_basis: bfloat16 [262144, 128], P('grid'), may hold values from -0.01171875 to 0.01171875
- seed_days: int32 [16], replicated, may hold values from 0 to 6143, as said below
Outputs:
- memberships: float32 [6144, 16], P('day')
- regime_centers: float32 [16, 128], replicated
- composites: float32 [16, 262144], P(None, 'grid')
The draws below stay inside these ranges and needn't reach their ends.
Inputs may be any that keep to these rules, and one draw needn't show every extreme that they name: `seed_days`: 16 distinct days of the record.
All inputs are finite; a program needn't handle non-finite values.
Results may differ from the reference program's by a relative error of at most 0.00043.
Values sent between devices are 32-bit elements; how exact they have to be, the bound alone decides.
No kernel may reach another device: no remote copies, remote signals or barrier semaphores. Data moves between devices by JAX's collectives and lax.ppermute only.
A program may use at most 32 MiB of HBM per device.

```python
import jax
import jax.numpy as jnp
from jax import lax

K = 128
C = 16
ITERS = 3
DAYS = 6144
G = 262144


def draw_fields(key, part):
    key_label = jax.random.fold_in(key, 11)
    key_pattern = jax.random.fold_in(key, 12)
    key_noise = jax.random.fold_in(key, 13)
    labels = jax.random.randint(key_label, (DAYS,), 0, C)
    patterns = jax.random.normal(key_pattern, (C, G), jnp.float32)
    noise = jax.random.normal(key_noise, (DAYS, G), jnp.float32)
    values = 1.5 * jnp.take(patterns, labels, axis=0) + noise
    return values.astype(jnp.bfloat16)


def draw_seed_days(key, part):
    inner = jax.random.permutation(jax.random.fold_in(key, 21), DAYS - 2)[:C - 2].astype(jnp.int32) + 1
    ends = jnp.array([0, DAYS - 1], dtype=jnp.int32)
    chosen = jnp.concatenate([ends, inner])
    order = jax.random.permutation(jax.random.fold_in(key, 22), C)
    return chosen[order].astype(jnp.int32)


def block_scale(own_key, dims, cuts, smallest, top_value):
    loudness = 1.0
    for dim, parts in cuts:
        heights = jax.random.uniform(jax.random.fold_in(jax.random.fold_in(own_key, 6), dim), (parts,), jnp.float32, smallest / len(cuts), top_value / len(cuts))
        loudness = loudness * jnp.repeat(jnp.exp(heights), dims[dim] // parts).reshape((-1,) + (1,) * (len(dims) - 1 - dim))
    return loudness


def bell_draw(own_key, extent, width, reach, shards=(), kind=jnp.bfloat16):
    values = width * jax.random.normal(own_key, extent, jnp.float32)
    if shards:
        values = values * block_scale(own_key, extent, shards, -0.22, 0.18)
    return jnp.clip(values, -reach, reach).astype(kind)


def setup_inputs(seed: int = 0) -> dict:
    arg_keys = jax.random.split(jax.random.key(seed), 4)
    fields = draw_fields(jax.random.fold_in(arg_keys[3], 71), 0)
    eof_basis = bell_draw(arg_keys[1], (G, K), G ** -0.5, 0.01171875, ((0, 64),))
    seed_days = draw_seed_days(jax.random.fold_in(arg_keys[3], 71), 0)
    return dict(fields=fields, eof_basis=eof_basis, seed_days=seed_days)


def member_of(amplitudes, centers):
    offsets = amplitudes[:, None, :] - centers[None, :, :]
    mean_square = jnp.mean(offsets * offsets, axis=2) + 1e-5
    weights = 1.0 / mean_square
    return weights / jnp.sum(weights, axis=1, keepdims=True)


def reference(fields, eof_basis, seed_days):
    amplitudes = jnp.dot(fields, eof_basis, preferred_element_type=jnp.float32)
    centers = jnp.take(amplitudes, seed_days.astype(jnp.int32), axis=0)
    for sweep in range(ITERS):
        member = member_of(amplitudes, centers)
        squared = member * member
        numerator = jnp.dot(squared.T, amplitudes, precision=lax.Precision.HIGHEST)
        centers = numerator / jnp.sum(squared, axis=0)[:, None]
    memberships = member_of(amplitudes, centers)
    squares = memberships * memberships
    weights_bf = squares.astype(jnp.bfloat16)
    numerator = jnp.dot(weights_bf.T, fields, preferred_element_type=jnp.float32)
    composites = numerator / jnp.sum(squares, axis=0)[:, None]
    return memberships, centers, composites
```

```python
import jax
import jax.numpy as jnp
from jax import lax
from jax.sharding import PartitionSpec as P

ITERS = 3
K = 128
C = 16


def member_of(amplitudes, centers):
    offsets = amplitudes[:, None, :] - centers[None, :, :]
    mean_square = jnp.mean(offsets * offsets, axis=2) + 1e-05
    weights = 1.0 / mean_square
    return weights / jnp.sum(weights, axis=1, keepdims=True)


def gather_all(value, axis, members):
    copies = jnp.broadcast_to(value[None], (members,) + value.shape)
    return lax.all_to_all(copies, axis, 0, 0)


def on_device(fields, eof_basis, seed_days, *, grids, days):
    rows, points = fields.shape
    partial_value = jnp.dot(fields, eof_basis, preferred_element_type=jnp.float32)
    pieces = lax.all_to_all(
        partial_value.reshape(grids, rows // grids, K), "grid", 0, 0
    )
    own = jnp.sum(pieces, axis=0)
    amplitudes = gather_all(own, "grid", grids).reshape(rows, K)

    first = lax.axis_index("day") * rows
    positions = first + jnp.arange(rows, dtype=jnp.int32)
    selector = (seed_days[:, None] == positions[None, :]).astype(jnp.float32)
    seeds = jnp.dot(selector, amplitudes, precision=lax.Precision.HIGHEST)
    centers = jnp.sum(gather_all(seeds, "day", days), axis=0)
    for sweep in range(ITERS):
        member = member_of(amplitudes, centers)
        squared = member * member
        numerator = jnp.dot(squared.T, amplitudes, precision=lax.Precision.HIGHEST)
        denominator = jnp.sum(squared, axis=0)
        terms = jnp.concatenate(
            [numerator, jnp.pad(denominator[None, :], ((0, 7), (0, K - C)))], axis=0
        )
        totals = jnp.sum(gather_all(terms, "day", days), axis=0)
        centers = totals[:C] / totals[C, :C][:, None]
    member_all = member_of(amplitudes, centers)
    squares = member_all * member_all
    weights_bf = squares.astype(jnp.bfloat16)
    weighted = jnp.dot(weights_bf.T, fields, preferred_element_type=jnp.float32)
    width = points // days
    pieces = lax.all_to_all(
        weighted.reshape(C, days, width).transpose(1, 0, 2), "day", 0, 0
    )
    own = jnp.sum(pieces, axis=0).reshape(C * width // K, K)
    weight_sums = jnp.pad(jnp.sum(squares, axis=0)[None, :], ((0, 7), (0, K - C)))
    both = gather_all(jnp.concatenate([own, weight_sums], axis=0), "day", days)
    whole = both[:, : C * width // K].reshape(days, C, width)
    totals = whole.transpose(1, 0, 2).reshape(C, points)
    weight_sums = jnp.sum(both[:, C * width // K, :C], axis=0)
    return (member_all, centers, totals / weight_sums[:, None])


def solution(mesh):
    placed = (P("day", "grid"), P("grid", None), P())

    def body(fields, eof_basis, seed_days):
        return on_device(
            fields,
            eof_basis,
            seed_days,
            grids=mesh.shape["grid"],
            days=mesh.shape["day"],
        )

    return jax.shard_map(
        body,
        mesh=mesh,
        in_specs=placed,
        out_specs=(P("day", None), P(), P(None, "grid")),
        check_vma=False,
    )
```

```python
import functools

import jax
import jax.numpy as jnp
from jax import lax
from jax.experimental import pallas as pl
from jax.experimental.pallas import tpu as pltpu
from jax.sharding import Mesh, PartitionSpec as P

ITERS = 3
K = 128
C = 16
STEPS = 4
HIGHEST = lax.Precision.HIGHEST


def call(kernel, out_shape, *args, name, cost=None):
    flops, moved = cost or (1000000, 500000)
    return pl.pallas_call(
        kernel,
        out_shape=out_shape,
        name=name,
        compiler_params=pltpu.CompilerParams(vmem_limit_bytes=8 << 20),
        cost_estimate=pl.CostEstimate(
            flops=flops, bytes_accessed=moved, transcendentals=0
        ),
    )(*args)


def row_of(column):
    lane = lax.broadcasted_iota(jnp.int32, (C, K), 1)
    sub = lax.broadcasted_iota(jnp.int32, (C, K), 0)
    return jnp.sum(jnp.where(lane == sub, column, 0.0), axis=0, keepdims=True)


def column_of(row):
    lane = lax.broadcasted_iota(jnp.int32, (C, K), 1)
    sub = lax.broadcasted_iota(jnp.int32, (C, K), 0)
    return jnp.sum(jnp.where(lane == sub, row, 0.0), axis=1, keepdims=True)


def member_rows(flipped, centers_flipped):
    sums = []
    for c in range(C):
        offset = flipped - centers_flipped[:, c : c + 1]
        sums.append(jnp.sum(offset * offset, axis=0, keepdims=True))
    mean_square = jnp.concatenate(sums, axis=0) / K + 1e-05
    weights = 1.0 / mean_square
    return weights / jnp.sum(weights, axis=0, keepdims=True)


def total_of(ref):
    total = ref[0]
    for i in range(1, ref.shape[0]):
        total = total + ref[i]
    return total


def centers_from(terms_ref):
    total = total_of(terms_ref)
    return total[:C, 0] / column_of(total[C])


def field_copies(fields_ref, chunks_ref, sem_ref):
    step = chunks_ref.shape[2]
    return [
        pltpu.make_async_copy(
            fields_ref.at[:, pl.ds(i * step, step)], chunks_ref.at[i], sem_ref.at[i]
        )
        for i in range(STEPS)
    ]


def project_kernel(fields_ref, basis_ref, out_ref, chunks_ref, basis_chunks_ref, sem_ref, basis_sem_ref):
    step = chunks_ref.shape[2]
    field_loads = field_copies(fields_ref, chunks_ref, sem_ref)
    basis_loads = [
        pltpu.make_async_copy(
            basis_ref.at[pl.ds(i * step, step)],
            basis_chunks_ref.at[i],
            basis_sem_ref.at[i],
        )
        for i in range(STEPS)
    ]
    for i in range(STEPS):
        basis_loads[i].start()
        field_loads[i].start()
    total = None
    for i in range(STEPS):
        basis_loads[i].wait()
        field_loads[i].wait()
        part = jnp.dot(
            chunks_ref[i], basis_chunks_ref[i], preferred_element_type=jnp.float32
        )
        total = part if total is None else total + part
    grids, own = out_ref.shape[:2]
    for r in range(own):
        out_ref[:, r, 0, :] = total[r * grids : (r + 1) * grids]


def project(fields, basis, grids):
    rows, points = fields.shape
    step = points // STEPS
    return pl.pallas_call(
        project_kernel,
        in_specs=[pl.BlockSpec(memory_space=pltpu.HBM)] * 2,
        out_shape=jax.ShapeDtypeStruct((grids, rows // grids, 1, K), jnp.float32),
        scratch_shapes=[
            pltpu.VMEM((STEPS, rows, step), jnp.bfloat16),
            pltpu.VMEM((STEPS, step, K), jnp.bfloat16),
            pltpu.SemaphoreType.DMA((STEPS,)),
            pltpu.SemaphoreType.DMA((STEPS,)),
        ],
        name="project",
        compiler_params=pltpu.CompilerParams(vmem_limit_bytes=63 << 20),
    )(fields, basis)


def own_rows_kernel(pieces_ref, out_ref):
    total = total_of(pieces_ref)
    out_ref[...] = jnp.broadcast_to(total[None], out_ref.shape)


def seeds_kernel(pieces_ref, wanted_ref, flipped_ref, seeds_ref):
    own = pieces_ref.shape[1]
    amplitudes = jnp.concatenate([pieces_ref[:, r, 0, :] for r in range(own)], axis=0)
    rows = amplitudes.shape[0]
    position = lax.broadcasted_iota(jnp.int32, (C, rows), 1)
    selector = (wanted_ref[...] == position).astype(jnp.float32)
    seeds = jnp.dot(
        selector, amplitudes, precision=HIGHEST, preferred_element_type=jnp.float32
    )
    flipped_ref[...] = amplitudes.T
    seeds_ref[...] = jnp.broadcast_to(seeds[None], seeds_ref.shape)


def store_terms(flipped, centers, out_ref):
    member = member_rows(flipped, centers.T)
    squared = member * member
    numerator = lax.dot_general(
        squared,
        flipped,
        (((1,), (1,)), ((), ())),
        precision=HIGHEST,
        preferred_element_type=jnp.float32,
    )
    weight_row = row_of(jnp.sum(squared, axis=1, keepdims=True))
    for i in range(out_ref.shape[0]):
        out_ref[i, :C, 0, :] = numerator
        out_ref[i, C, :, :] = weight_row


def first_kernel(core_ref, seeds_ref, flipped_ref, other_ref, out_ref, chip_ref):
    rows = flipped_ref.shape[1]

    @pl.when(core_ref[0] == 0)
    def _():
        chip_ref[:, :rows] = flipped_ref[...]
        chip_ref[:, rows:] = other_ref[...]

    @pl.when(core_ref[0] != 0)
    def _():
        chip_ref[:, :rows] = other_ref[...]
        chip_ref[:, rows:] = flipped_ref[...]

    store_terms(chip_ref[...], total_of(seeds_ref), out_ref)


def first_terms(core, seeds, flipped, other, layers):
    rows = flipped.shape[1]
    return pl.pallas_call(
        first_kernel,
        in_specs=[pl.BlockSpec(memory_space=pltpu.SMEM)]
        + [pl.BlockSpec(memory_space=pltpu.VMEM)] * 3,
        out_shape=[
            jax.ShapeDtypeStruct((layers, C + 1, 1, K), jnp.float32),
            jax.ShapeDtypeStruct((K, 2 * rows), jnp.float32),
        ],
        name="first",
        compiler_params=pltpu.CompilerParams(vmem_limit_bytes=8 << 20),
    )(core, seeds, flipped, other)


def sweep_kernel(terms_ref, flipped_ref, out_ref):
    store_terms(flipped_ref[...], centers_from(terms_ref), out_ref)


def weigh_kernel(
    terms_ref,
    flipped_ref,
    fields_ref,
    member_ref,
    centers_ref,
    row_ref,
    out_ref,
    chunks_ref,
    sem_ref,
):
    loads = field_copies(fields_ref, chunks_ref, sem_ref)
    for load in loads:
        load.start()
    centers = centers_from(terms_ref)
    centers_ref[...] = centers
    member = member_rows(flipped_ref[...], centers.T)
    member_ref[...] = member
    squares = member * member
    row_ref[...] = row_of(jnp.sum(squares, axis=1, keepdims=True))
    weights_bf = squares.astype(jnp.bfloat16)
    width = out_ref.shape[2]
    each = out_ref.shape[0] // STEPS
    for i in range(STEPS):
        loads[i].wait()
        part = jnp.dot(weights_bf, chunks_ref[i], preferred_element_type=jnp.float32)
        for j in range(each):
            out_ref[i * each + j] = part[:, j * width : (j + 1) * width]


def weigh(terms, flipped, fields, days):
    rows, points = fields.shape
    vmem = pl.BlockSpec(memory_space=pltpu.VMEM)
    return pl.pallas_call(
        weigh_kernel,
        in_specs=[vmem, vmem, pl.BlockSpec(memory_space=pltpu.HBM)],
        out_shape=[
            jax.ShapeDtypeStruct((C, rows), jnp.float32),
            jax.ShapeDtypeStruct((C, K), jnp.float32),
            jax.ShapeDtypeStruct((1, K), jnp.float32),
            jax.ShapeDtypeStruct((days, C, points // days), jnp.float32),
        ],
        scratch_shapes=[
            pltpu.VMEM((STEPS, rows, points // STEPS), jnp.bfloat16),
            pltpu.SemaphoreType.DMA((STEPS,)),
        ],
        name="weigh",
        compiler_params=pltpu.CompilerParams(vmem_limit_bytes=62 << 20),
    )(terms, flipped, fields)


def own_points_kernel(pieces_ref, row_ref, out_ref):
    total = total_of(pieces_ref)
    tiles = total.shape[1] // K
    for i in range(out_ref.shape[0]):
        for t in range(tiles):
            out_ref[i, t * C : (t + 1) * C, 0, :] = total[:, t * K : (t + 1) * K]
        out_ref[i, tiles * C, :, :] = row_ref[...]


def finish_kernel(pieces_ref, out_ref):
    days, last = pieces_ref.shape[0], pieces_ref.shape[1] - 1
    weight_row = pieces_ref[0, last]
    for j in range(1, days):
        weight_row = weight_row + pieces_ref[j, last]
    weight = column_of(weight_row)
    tiles = last // C
    for j in range(days):
        for t in range(tiles):
            at = (j * tiles + t) * K
            out_ref[:, at : at + K] = pieces_ref[j, t * C : (t + 1) * C, 0, :] / weight


def on_device(fields, eof_basis, seed_days, *, grids, layers):
    rows, points = fields.shape
    days = 2 * layers
    f32 = jnp.float32
    own = rows // grids
    both = ("z", "c")

    def exchange(value, axis):
        return lax.all_to_all(value, axis, 0, 0)

    pieces = exchange(project(fields, eof_basis, grids), "grid")
    shape = jax.ShapeDtypeStruct((grids, own, 1, K), f32)
    pieces = exchange(call(own_rows_kernel, shape, pieces, name="own_rows"), "grid")

    core = lax.axis_index("c")
    first = (2 * lax.axis_index("z") + core) * rows
    flipped, seeds = call(
        seeds_kernel,
        [
            jax.ShapeDtypeStruct((K, rows), f32),
            jax.ShapeDtypeStruct((days, C, K), f32),
        ],
        pieces,
        (seed_days - first)[:, None],
        name="seeds",
    )
    other = lax.ppermute(flipped, "c", [(0, 1), (1, 0)])
    seeds = exchange(seeds, both)
    terms, chip = first_terms(core[None], seeds, flipped, other, layers)
    terms = exchange(terms, "z")
    shape = jax.ShapeDtypeStruct((layers, C + 1, 1, K), f32)
    for sweep in range(1, ITERS):
        terms = exchange(call(sweep_kernel, shape, terms, chip, name="sweep"), "z")

    member, centers, weight_row, weighted = weigh(terms, flipped, fields, days)
    pieces = exchange(weighted, both)
    tiles = points // days // K
    shape = jax.ShapeDtypeStruct((days, tiles * C + 1, 1, K), f32)
    pieces = call(own_points_kernel, shape, pieces, weight_row, name="own_points")
    pieces = exchange(pieces, both)
    shape = jax.ShapeDtypeStruct((C, points), f32)
    composites = call(finish_kernel, shape, pieces, name="finish")
    return (member.T, centers, composites)


def solution(mesh):
    grids, days = mesh.shape["grid"], mesh.shape["day"]
    finer = Mesh(mesh.devices.reshape(grids, days // 2, 2), ("grid", "z", "c"))
    both = ("z", "c")
    return jax.shard_map(
        functools.partial(on_device, grids=grids, layers=days // 2),
        mesh=finer,
        in_specs=(P(both, "grid"), P("grid", None), P()),
        out_specs=(P(both, None), P(), P(None, "grid")),
        check_vma=False,
    )
```

```python
import functools

import jax
import jax.numpy as jnp
from jax import lax
from jax.experimental import pallas as pl
from jax.experimental.pallas import tpu as pltpu
from jax.sharding import PartitionSpec as P

ITERS = 3
K = 128
C = 16
BLOCKS = 3
PARTS = 4
HIGHEST = lax.Precision.HIGHEST


def call(kernel, out_shape, *args, name, cost=None):
    flops, moved = cost or (1000000, 500000)
    return pl.pallas_call(
        kernel,
        out_shape=out_shape,
        name=name,
        compiler_params=pltpu.CompilerParams(vmem_limit_bytes=8 << 20),
        cost_estimate=pl.CostEstimate(
            flops=flops, bytes_accessed=moved, transcendentals=0
        ),
    )(*args)


def row_of(column):
    lane = lax.broadcasted_iota(jnp.int32, (C, K), 1)
    sub = lax.broadcasted_iota(jnp.int32, (C, K), 0)
    return jnp.sum(jnp.where(lane == sub, column, 0.0), axis=0, keepdims=True)


def column_of(row):
    lane = lax.broadcasted_iota(jnp.int32, (C, K), 1)
    sub = lax.broadcasted_iota(jnp.int32, (C, K), 0)
    return jnp.sum(jnp.where(lane == sub, row, 0.0), axis=1, keepdims=True)


def member_rows(flipped, centers_flipped):
    sums = []
    for c in range(C):
        offset = flipped - centers_flipped[:, c : c + 1]
        sums.append(jnp.sum(offset * offset, axis=0, keepdims=True))
    mean_square = jnp.concatenate(sums, axis=0) / K + 1e-05
    weights = 1.0 / mean_square
    return weights / jnp.sum(weights, axis=0, keepdims=True)


def total_of(ref):
    total = ref[0]
    for i in range(1, ref.shape[0]):
        total = total + ref[i]
    return total


def centers_from(terms_ref):
    total = total_of(terms_ref)
    return total[:C, 0] / column_of(total[C])


def project_kernel(
    fields_ref, basis_ref, out_ref, chunks_ref, basis_chunks_ref, sem_ref, basis_sem_ref
):
    blocks, rows = chunks_ref.shape[:2]
    parts, step = basis_chunks_ref.shape[:2]
    basis_loads = [
        pltpu.make_async_copy(
            basis_ref.at[pl.ds(j * step, step)],
            basis_chunks_ref.at[j],
            basis_sem_ref.at[j],
        )
        for j in range(parts)
    ]
    loads = [
        pltpu.make_async_copy(
            fields_ref.at[pl.ds(i * rows, rows)], chunks_ref.at[i], sem_ref.at[i]
        )
        for i in range(blocks)
    ]
    for load in basis_loads + loads:
        load.start()
    for load in basis_loads:
        load.wait()
    grids = out_ref.shape[0]
    for i in range(blocks):
        loads[i].wait()
        total = None
        for j in range(parts):
            part = jnp.dot(
                chunks_ref[i, :, j * step : (j + 1) * step],
                basis_chunks_ref[j],
                preferred_element_type=jnp.float32,
            )
            total = part if total is None else total + part
        each = rows // grids
        for r in range(each):
            out_ref[:, i * each + r, 0, :] = total[r * grids : (r + 1) * grids]


def project(fields, basis, grids):
    rows, points = fields.shape
    return pl.pallas_call(
        project_kernel,
        in_specs=[pl.BlockSpec(memory_space=pltpu.HBM)] * 2,
        out_shape=jax.ShapeDtypeStruct((grids, rows // grids, 1, K), jnp.float32),
        scratch_shapes=[
            pltpu.VMEM((BLOCKS, rows // BLOCKS, points), jnp.bfloat16),
            pltpu.VMEM((PARTS, points // PARTS, K), jnp.bfloat16),
            pltpu.SemaphoreType.DMA((BLOCKS,)),
            pltpu.SemaphoreType.DMA((PARTS,)),
        ],
        name="project",
        compiler_params=pltpu.CompilerParams(vmem_limit_bytes=63 << 20),
    )(fields, basis)


def own_rows_kernel(pieces_ref, out_ref):
    total = total_of(pieces_ref)
    out_ref[...] = jnp.broadcast_to(total[None], out_ref.shape)


def seeds_kernel(days_ref, pieces_ref, flipped_ref, seeds_ref):
    own = pieces_ref.shape[1]
    amplitudes = jnp.concatenate([pieces_ref[:, r, 0, :] for r in range(own)], axis=0)
    rows = amplitudes.shape[0]
    first = lax.axis_index("day") * rows
    position = first + lax.broadcasted_iota(jnp.int32, (1, rows), 1)
    selector = jnp.concatenate(
        [(position == days_ref[c]).astype(jnp.float32) for c in range(C)], axis=0
    )
    seeds = jnp.dot(
        selector, amplitudes, precision=HIGHEST, preferred_element_type=jnp.float32
    )
    flipped_ref[...] = amplitudes.T
    seeds_ref[...] = jnp.broadcast_to(seeds[None], seeds_ref.shape)


def store_terms(flipped, centers, out_ref):
    member = member_rows(flipped, centers.T)
    squared = member * member
    numerator = lax.dot_general(
        squared,
        flipped,
        (((1,), (1,)), ((), ())),
        precision=HIGHEST,
        preferred_element_type=jnp.float32,
    )
    weight_row = row_of(jnp.sum(squared, axis=1, keepdims=True))
    for i in range(out_ref.shape[0]):
        out_ref[i, :C, 0, :] = numerator
        out_ref[i, C, :, :] = weight_row


def first_kernel(seeds_ref, flipped_ref, out_ref):
    store_terms(flipped_ref[...], total_of(seeds_ref), out_ref)


def sweep_kernel(terms_ref, flipped_ref, out_ref):
    store_terms(flipped_ref[...], centers_from(terms_ref), out_ref)


def weigh_kernel(
    terms_ref, flipped_ref, fields_ref, member_ref, centers_ref, row_ref, out_ref
):
    centers = centers_from(terms_ref)
    centers_ref[...] = centers
    member = member_rows(flipped_ref[...], centers.T)
    member_ref[...] = member
    squares = member * member
    row_ref[...] = row_of(jnp.sum(squares, axis=1, keepdims=True))
    weights_bf = squares.astype(jnp.bfloat16)
    days, _, width = out_ref.shape
    for j in range(days):
        out_ref[j] = jnp.dot(
            weights_bf,
            fields_ref[:, j * width : (j + 1) * width],
            preferred_element_type=jnp.float32,
        )


def own_points_kernel(pieces_ref, row_ref, out_ref):
    total = total_of(pieces_ref)
    tiles = total.shape[1] // K
    for i in range(out_ref.shape[0]):
        for t in range(tiles):
            out_ref[i, t * C : (t + 1) * C, 0, :] = total[:, t * K : (t + 1) * K]
        out_ref[i, tiles * C, :, :] = row_ref[...]


def finish_kernel(pieces_ref, out_ref):
    days, last = pieces_ref.shape[0], pieces_ref.shape[1] - 1
    weight_row = pieces_ref[0, last]
    for j in range(1, days):
        weight_row = weight_row + pieces_ref[j, last]
    weight = column_of(weight_row)
    tiles = last // C
    for j in range(days):
        for t in range(tiles):
            at = (j * tiles + t) * K
            out_ref[:, at : at + K] = pieces_ref[j, t * C : (t + 1) * C, 0, :] / weight


def on_device(fields, eof_basis, seed_days, *, grids, days):
    rows, points = fields.shape
    f32 = jnp.float32
    own = rows // grids

    def exchange(value, axis):
        return lax.all_to_all(value, axis, 0, 0)

    pieces = exchange(project(fields, eof_basis, grids), "grid")
    shape = jax.ShapeDtypeStruct((grids, own, 1, K), f32)
    pieces = exchange(call(own_rows_kernel, shape, pieces, name="own_rows"), "grid")

    smem = pl.BlockSpec(memory_space=pltpu.SMEM)
    flipped, seeds = pl.pallas_call(
        seeds_kernel,
        in_specs=[smem, pl.BlockSpec(memory_space=pltpu.VMEM)],
        out_shape=[
            jax.ShapeDtypeStruct((K, rows), f32),
            jax.ShapeDtypeStruct((days, C, K), f32),
        ],
        name="seeds",
        compiler_params=pltpu.CompilerParams(vmem_limit_bytes=8 << 20),
    )(seed_days, pieces)
    seeds = exchange(seeds, "day")
    shape = jax.ShapeDtypeStruct((days, C + 1, 1, K), f32)
    terms = exchange(call(first_kernel, shape, seeds, flipped, name="first"), "day")
    for sweep in range(1, ITERS):
        terms = call(sweep_kernel, shape, terms, flipped, name="sweep")
        terms = exchange(terms, "day")

    shapes = [
        jax.ShapeDtypeStruct((C, rows), f32),
        jax.ShapeDtypeStruct((C, K), f32),
        jax.ShapeDtypeStruct((1, K), f32),
        jax.ShapeDtypeStruct((days, C, points // days), f32),
    ]
    member, centers, weight_row, weighted = call(
        weigh_kernel, shapes, terms, flipped, fields, name="weigh"
    )
    pieces = exchange(weighted, "day")
    tiles = points // days // K
    shape = jax.ShapeDtypeStruct((days, tiles * C + 1, 1, K), f32)
    pieces = call(own_points_kernel, shape, pieces, weight_row, name="own_points")
    pieces = exchange(pieces, "day")
    shape = jax.ShapeDtypeStruct((C, points), f32)
    composites = call(finish_kernel, shape, pieces, name="finish")
    return (member.T, centers, composites)


def solution(mesh):
    return jax.shard_map(
        functools.partial(
            on_device, grids=mesh.shape["grid"], days=mesh.shape["day"]
        ),
        mesh=mesh,
        in_specs=(P("day", "grid"), P("grid", None), P()),
        out_specs=(P("day", None), P(), P(None, "grid")),
        check_vma=False,
    )
```

```python
import functools

import jax
import jax.numpy as jnp
from jax import lax
from jax.experimental import pallas as pl
from jax.experimental.pallas import tpu as pltpu
from jax.sharding import PartitionSpec as P

ITERS = 3
K = 128
C = 16
BLOCKS = 3
PARTS = 4
GROUP = 8
HIGHEST = lax.Precision.HIGHEST


def call(kernel, out_shape, *args, name, cost=None):
    flops, moved = cost or (1000000, 500000)
    return pl.pallas_call(
        kernel,
        out_shape=out_shape,
        name=name,
        compiler_params=pltpu.CompilerParams(vmem_limit_bytes=8 << 20),
        cost_estimate=pl.CostEstimate(
            flops=flops, bytes_accessed=moved, transcendentals=0
        ),
    )(*args)


def row_of(column):
    lane = lax.broadcasted_iota(jnp.int32, (C, K), 1)
    sub = lax.broadcasted_iota(jnp.int32, (C, K), 0)
    return jnp.sum(jnp.where(lane == sub, column, 0.0), axis=0, keepdims=True)


def column_of(row):
    lane = lax.broadcasted_iota(jnp.int32, (C, K), 1)
    sub = lax.broadcasted_iota(jnp.int32, (C, K), 0)
    return jnp.sum(jnp.where(lane == sub, row, 0.0), axis=1, keepdims=True)


def member_rows(flipped, centers_flipped):
    sums = []
    for c in range(C):
        offset = flipped - centers_flipped[:, c : c + 1]
        sums.append(jnp.sum(offset * offset, axis=0, keepdims=True))
    mean_square = jnp.concatenate(sums, axis=0) / K + 1e-05
    weights = 1.0 / mean_square
    return weights / jnp.sum(weights, axis=0, keepdims=True)


def total_of(ref):
    total = ref[0]
    for i in range(1, ref.shape[0]):
        total = total + ref[i]
    return total


def centers_from(terms_ref):
    total = total_of(terms_ref)
    return total[:C, 0] / column_of(total[C])


def early_kernel(
    days_ref, fields_ref, basis_ref, out_ref, groups_ref, chunk_ref, sem_ref, basis_sem_ref
):
    rows = fields_ref.shape[0]
    first = lax.axis_index("day") * rows
    basis_load = pltpu.make_async_copy(basis_ref, chunk_ref, basis_sem_ref)
    basis_load.start()
    lane = lax.broadcasted_iota(jnp.int32, (1, C * GROUP), 1)
    loads, picks = [], []
    for c in range(C):
        row = days_ref[c] - first
        inside = jnp.logical_and(row >= 0, row < rows)
        near = jnp.clip(row, 0, rows - 1)
        within = lax.rem(near, GROUP)
        start = pl.multiple_of(near - within, GROUP)
        loads.append(
            pltpu.make_async_copy(
                fields_ref.at[pl.ds(start, GROUP)],
                groups_ref.at[pl.ds(c * GROUP, GROUP)],
                sem_ref.at[c],
            )
        )
        loads[-1].start()
        wanted = jnp.where(inside, c * GROUP + within, -1)
        picks.append((lane == wanted).astype(jnp.float32))
    selector = jnp.concatenate(picks, axis=0).astype(jnp.bfloat16)
    for load in loads:
        load.wait()
    chosen = jnp.dot(selector, groups_ref[...], preferred_element_type=jnp.float32)
    basis_load.wait()
    seeds = jnp.dot(
        chosen.astype(jnp.bfloat16), chunk_ref[...], preferred_element_type=jnp.float32
    )
    out_ref[...] = jnp.broadcast_to(seeds[None], out_ref.shape)


def early_seeds(seed_days, fields, basis, days):
    points = fields.shape[1]
    hbm = pl.BlockSpec(memory_space=pltpu.HBM)
    return pl.pallas_call(
        early_kernel,
        in_specs=[pl.BlockSpec(memory_space=pltpu.SMEM), hbm, hbm],
        out_shape=jax.ShapeDtypeStruct((days, C, K), jnp.float32),
        scratch_shapes=[
            pltpu.VMEM((C * GROUP, points), jnp.bfloat16),
            pltpu.VMEM((points, K), jnp.bfloat16),
            pltpu.SemaphoreType.DMA((C,)),
            pltpu.SemaphoreType.DMA,
        ],
        name="early_seeds",
        compiler_params=pltpu.CompilerParams(vmem_limit_bytes=63 << 20),
    )(seed_days, fields, basis)


def project_kernel(
    fields_ref, basis_ref, out_ref, chunks_ref, basis_chunks_ref, sem_ref, basis_sem_ref
):
    blocks, rows = chunks_ref.shape[:2]
    parts, step = basis_chunks_ref.shape[:2]
    basis_loads = [
        pltpu.make_async_copy(
            basis_ref.at[pl.ds(j * step, step)],
            basis_chunks_ref.at[j],
            basis_sem_ref.at[j],
        )
        for j in range(parts)
    ]
    loads = [
        pltpu.make_async_copy(
            fields_ref.at[pl.ds(i * rows, rows)], chunks_ref.at[i], sem_ref.at[i]
        )
        for i in range(blocks)
    ]
    for load in basis_loads + loads:
        load.start()
    for load in basis_loads:
        load.wait()
    for i in range(blocks):
        loads[i].wait()
        total = None
        for j in range(parts):
            part = jnp.dot(
                chunks_ref[i, :, j * step : (j + 1) * step],
                basis_chunks_ref[j],
                preferred_element_type=jnp.float32,
            )
            total = part if total is None else total + part
        out_ref[i * rows : (i + 1) * rows, :] = total


def project(fields, basis):
    rows, points = fields.shape
    return pl.pallas_call(
        project_kernel,
        in_specs=[pl.BlockSpec(memory_space=pltpu.HBM)] * 2,
        out_shape=jax.ShapeDtypeStruct((rows, K), jnp.float32),
        scratch_shapes=[
            pltpu.VMEM((BLOCKS, rows // BLOCKS, points), jnp.bfloat16),
            pltpu.VMEM((PARTS, points // PARTS, K), jnp.bfloat16),
            pltpu.SemaphoreType.DMA((BLOCKS,)),
            pltpu.SemaphoreType.DMA((PARTS,)),
        ],
        name="project",
        cost_estimate=pl.CostEstimate(
            flops=2 * rows * points * K,
            bytes_accessed=2 * points * (rows + K) + 4 * rows * K,
            transcendentals=0,
        ),
        compiler_params=pltpu.CompilerParams(vmem_limit_bytes=63 << 20),
    )(fields, basis)


def pack_kernel(partial_ref, seeds_ref, out_ref):
    grids, own = out_ref.shape[0], out_ref.shape[1] - 1
    for r in range(own):
        out_ref[:, r, 0, :] = partial_ref[r * grids : (r + 1) * grids, :]
    seeds = total_of(seeds_ref)
    shares = grids // C
    lane = lax.broadcasted_iota(jnp.int32, (C, K), 1)
    for q in range(shares):
        mine = jnp.logical_and(lane >= q * K // shares, lane < (q + 1) * K // shares)
        out_ref[pl.ds(q, C, stride=shares), own, 0, :] = jnp.where(mine, seeds, 0.0)


def own_rows_kernel(pieces_ref, out_ref):
    total = total_of(pieces_ref)
    out_ref[...] = jnp.broadcast_to(total[None], out_ref.shape)


def store_terms(flipped, centers, out_ref):
    member = member_rows(flipped, centers.T)
    squared = member * member
    numerator = lax.dot_general(
        squared,
        flipped,
        (((1,), (1,)), ((), ())),
        precision=HIGHEST,
        preferred_element_type=jnp.float32,
    )
    weight_row = row_of(jnp.sum(squared, axis=1, keepdims=True))
    for i in range(out_ref.shape[0]):
        out_ref[i, :C, 0, :] = numerator
        out_ref[i, C, :, :] = weight_row


def first_kernel(pieces_ref, flipped_ref, out_ref):
    grids, own = pieces_ref.shape[0], pieces_ref.shape[1] - 1
    amplitudes = jnp.concatenate([pieces_ref[:, r, 0, :] for r in range(own)], axis=0)
    flipped = amplitudes.T
    flipped_ref[...] = flipped
    shares = grids // C
    centers = pieces_ref[pl.ds(0, C, stride=shares), own, 0, :]
    for q in range(1, shares):
        centers = centers + pieces_ref[pl.ds(q, C, stride=shares), own, 0, :]
    store_terms(flipped, centers, out_ref)


def sweep_kernel(terms_ref, flipped_ref, out_ref):
    store_terms(flipped_ref[...], centers_from(terms_ref), out_ref)


def weigh_kernel(
    terms_ref, flipped_ref, fields_ref, member_ref, centers_ref, row_ref, out_ref
):
    centers = centers_from(terms_ref)
    centers_ref[...] = centers
    member = member_rows(flipped_ref[...], centers.T)
    member_ref[...] = member
    squares = member * member
    row_ref[...] = row_of(jnp.sum(squares, axis=1, keepdims=True))
    weights_bf = squares.astype(jnp.bfloat16)
    days, _, width = out_ref.shape
    for j in range(days):
        out_ref[j] = jnp.dot(
            weights_bf,
            fields_ref[:, j * width : (j + 1) * width],
            preferred_element_type=jnp.float32,
        )


def own_points_kernel(pieces_ref, row_ref, out_ref):
    total = total_of(pieces_ref)
    tiles = total.shape[1] // K
    for i in range(out_ref.shape[0]):
        for t in range(tiles):
            out_ref[i, t * C : (t + 1) * C, 0, :] = total[:, t * K : (t + 1) * K]
        out_ref[i, tiles * C, :, :] = row_ref[...]


def finish_kernel(pieces_ref, out_ref):
    days, last = pieces_ref.shape[0], pieces_ref.shape[1] - 1
    weight_row = pieces_ref[0, last]
    for j in range(1, days):
        weight_row = weight_row + pieces_ref[j, last]
    weight = column_of(weight_row)
    tiles = last // C
    for j in range(days):
        for t in range(tiles):
            at = (j * tiles + t) * K
            out_ref[:, at : at + K] = pieces_ref[j, t * C : (t + 1) * C, 0, :] / weight


def on_device(fields, eof_basis, seed_days, *, grids, days):
    rows, points = fields.shape
    f32 = jnp.float32
    own = rows // grids

    def exchange(value, axis):
        return lax.all_to_all(value, axis, 0, 0)

    seeds = exchange(early_seeds(seed_days, fields, eof_basis, days), "day")
    partial_value = project(fields, eof_basis)
    shape = jax.ShapeDtypeStruct((grids, own + 1, 1, K), f32)
    pieces = exchange(call(pack_kernel, shape, partial_value, seeds, name="pack"), "grid")
    pieces = exchange(call(own_rows_kernel, shape, pieces, name="own_rows"), "grid")
    shape = jax.ShapeDtypeStruct((days, C + 1, 1, K), f32)
    flipped, terms = call(
        first_kernel,
        [jax.ShapeDtypeStruct((K, rows), f32), shape],
        pieces,
        name="first",
    )
    terms = exchange(terms, "day")
    for sweep in range(1, ITERS):
        terms = call(sweep_kernel, shape, terms, flipped, name="sweep")
        terms = exchange(terms, "day")

    shapes = [
        jax.ShapeDtypeStruct((C, rows), f32),
        jax.ShapeDtypeStruct((C, K), f32),
        jax.ShapeDtypeStruct((1, K), f32),
        jax.ShapeDtypeStruct((days, C, points // days), f32),
    ]
    member, centers, weight_row, weighted = call(
        weigh_kernel, shapes, terms, flipped, fields, name="weigh"
    )
    pieces = exchange(weighted, "day")
    tiles = points // days // K
    shape = jax.ShapeDtypeStruct((days, tiles * C + 1, 1, K), f32)
    pieces = call(own_points_kernel, shape, pieces, weight_row, name="own_points")
    pieces = exchange(pieces, "day")
    shape = jax.ShapeDtypeStruct((C, points), f32)
    composites = call(finish_kernel, shape, pieces, name="finish")
    return (member.T, centers, composites)


def solution(mesh):
    return jax.shard_map(
        functools.partial(
            on_device, grids=mesh.shape["grid"], days=mesh.shape["day"]
        ),
        mesh=mesh,
        in_specs=(P("day", "grid"), P("grid", None), P()),
        out_specs=(P("day", None), P(), P(None, "grid")),
        check_vma=False,
    )
```

```python
import functools

import jax
import jax.numpy as jnp
from jax import lax
from jax.experimental import pallas as pl
from jax.experimental.pallas import tpu as pltpu
from jax.sharding import PartitionSpec as P

ITERS = 3
K = 128
C = 16
BLOCKS = 3
PARTS = 4
HIGHEST = lax.Precision.HIGHEST


def call(kernel, out_shape, *args, name, cost=None):
    flops, moved = cost or (1000000, 500000)
    return pl.pallas_call(
        kernel,
        out_shape=out_shape,
        name=name,
        compiler_params=pltpu.CompilerParams(vmem_limit_bytes=8 << 20),
        cost_estimate=pl.CostEstimate(
            flops=flops, bytes_accessed=moved, transcendentals=0
        ),
    )(*args)


def row_of(column):
    lane = lax.broadcasted_iota(jnp.int32, (C, K), 1)
    sub = lax.broadcasted_iota(jnp.int32, (C, K), 0)
    return jnp.sum(jnp.where(lane == sub, column, 0.0), axis=0, keepdims=True)


def column_of(row):
    lane = lax.broadcasted_iota(jnp.int32, (C, K), 1)
    sub = lax.broadcasted_iota(jnp.int32, (C, K), 0)
    return jnp.sum(jnp.where(lane == sub, row, 0.0), axis=1, keepdims=True)


def member_rows(flipped, centers_flipped):
    sums = []
    for c in range(C):
        offset = flipped - centers_flipped[:, c : c + 1]
        sums.append(jnp.sum(offset * offset, axis=0, keepdims=True))
    mean_square = jnp.concatenate(sums, axis=0) / K + 1e-05
    weights = 1.0 / mean_square
    return weights / jnp.sum(weights, axis=0, keepdims=True)


def total_of(ref):
    total = ref[0]
    for i in range(1, ref.shape[0]):
        total = total + ref[i]
    return total


def centers_from(terms_ref):
    total = total_of(terms_ref)
    return total[:C, 0] / column_of(total[C])


def project_kernel(
    fields_ref, basis_ref, out_ref, chunks_ref, basis_chunks_ref, sem_ref, basis_sem_ref
):
    blocks, rows = chunks_ref.shape[:2]
    parts, step = basis_chunks_ref.shape[:2]
    basis_loads = [
        pltpu.make_async_copy(
            basis_ref.at[pl.ds(j * step, step)],
            basis_chunks_ref.at[j],
            basis_sem_ref.at[j],
        )
        for j in range(parts)
    ]
    loads = [
        pltpu.make_async_copy(
            fields_ref.at[pl.ds(i * rows, rows)], chunks_ref.at[i], sem_ref.at[i]
        )
        for i in range(blocks)
    ]
    for load in basis_loads + loads:
        load.start()
    for load in basis_loads:
        load.wait()
    grids = out_ref.shape[0]
    for i in range(blocks):
        loads[i].wait()
        total = None
        for j in range(parts):
            part = jnp.dot(
                chunks_ref[i, :, j * step : (j + 1) * step],
                basis_chunks_ref[j],
                preferred_element_type=jnp.float32,
            )
            total = part if total is None else total + part
        each = rows // grids
        for r in range(each):
            out_ref[:, i * each + r, 0, :] = total[r * grids : (r + 1) * grids]


def project(fields, basis, grids):
    rows, points = fields.shape
    fields = pltpu.with_memory_space_constraint(fields, pltpu.HBM)
    basis = pltpu.with_memory_space_constraint(basis, pltpu.HBM)
    return pl.pallas_call(
        project_kernel,
        in_specs=[pl.BlockSpec(memory_space=pltpu.HBM)] * 2,
        out_specs=[pl.BlockSpec(memory_space=pltpu.VMEM)] * 2,
        out_shape=[
            jax.ShapeDtypeStruct((grids, rows // grids, 1, K), jnp.float32),
            jax.ShapeDtypeStruct((BLOCKS, rows // BLOCKS, points), jnp.bfloat16),
        ],
        scratch_shapes=[
            pltpu.VMEM((PARTS, points // PARTS, K), jnp.bfloat16),
            pltpu.SemaphoreType.DMA((BLOCKS,)),
            pltpu.SemaphoreType.DMA((PARTS,)),
        ],
        name="project",
        cost_estimate=pl.CostEstimate(
            flops=2 * rows * points * K,
            bytes_accessed=2 * points * (rows + K) + 4 * rows * K,
            transcendentals=0,
        ),
        compiler_params=pltpu.CompilerParams(vmem_limit_bytes=16 << 20),
    )(fields, basis)


def own_rows_kernel(pieces_ref, out_ref):
    total = total_of(pieces_ref)
    out_ref[...] = jnp.broadcast_to(total[None], out_ref.shape)


def seeds_kernel(days_ref, pieces_ref, flipped_ref, seeds_ref):
    own = pieces_ref.shape[1]
    amplitudes = jnp.concatenate([pieces_ref[:, r, 0, :] for r in range(own)], axis=0)
    rows = amplitudes.shape[0]
    first = lax.axis_index("day") * rows
    position = first + lax.broadcasted_iota(jnp.int32, (1, rows), 1)
    lane = lax.broadcasted_iota(jnp.int32, (C, C), 1)
    sub = lax.broadcasted_iota(jnp.int32, (C, C), 0)
    days = jnp.where(lane == sub, days_ref[...].astype(jnp.float32), 0.0)
    wanted = jnp.sum(days, axis=1, keepdims=True)
    selector = (position.astype(jnp.float32) == wanted).astype(jnp.float32)
    seeds = jnp.dot(
        selector, amplitudes, precision=HIGHEST, preferred_element_type=jnp.float32
    )
    flipped_ref[...] = amplitudes.T
    seeds_ref[...] = jnp.broadcast_to(seeds[None], seeds_ref.shape)


def store_terms(flipped, centers, out_ref):
    member = member_rows(flipped, centers.T)
    squared = member * member
    numerator = lax.dot_general(
        squared,
        flipped,
        (((1,), (1,)), ((), ())),
        precision=HIGHEST,
        preferred_element_type=jnp.float32,
    )
    weight_row = row_of(jnp.sum(squared, axis=1, keepdims=True))
    for i in range(out_ref.shape[0]):
        out_ref[i, :C, 0, :] = numerator
        out_ref[i, C, :, :] = weight_row


def first_kernel(seeds_ref, flipped_ref, out_ref):
    store_terms(flipped_ref[...], total_of(seeds_ref), out_ref)


def sweep_kernel(terms_ref, flipped_ref, out_ref):
    store_terms(flipped_ref[...], centers_from(terms_ref), out_ref)


def weigh_kernel(
    terms_ref, flipped_ref, fields_ref, member_ref, centers_ref, row_ref, out_ref
):
    centers = centers_from(terms_ref)
    centers_ref[...] = centers
    member = member_rows(flipped_ref[...], centers.T)
    member_ref[...] = member
    squares = member * member
    row_ref[...] = row_of(jnp.sum(squares, axis=1, keepdims=True))
    weights_bf = squares.astype(jnp.bfloat16)
    days, _, width = out_ref.shape
    for j in range(days):
        out_ref[j] = jnp.dot(
            weights_bf,
            fields_ref[:, j * width : (j + 1) * width],
            preferred_element_type=jnp.float32,
        )


def own_points_kernel(pieces_ref, row_ref, out_ref):
    total = total_of(pieces_ref)
    tiles = total.shape[1] // K
    for i in range(out_ref.shape[0]):
        for t in range(tiles):
            out_ref[i, t * C : (t + 1) * C, 0, :] = total[:, t * K : (t + 1) * K]
        out_ref[i, tiles * C, :, :] = row_ref[...]


def finish_kernel(pieces_ref, out_ref):
    days, last = pieces_ref.shape[0], pieces_ref.shape[1] - 1
    weight_row = pieces_ref[0, last]
    for j in range(1, days):
        weight_row = weight_row + pieces_ref[j, last]
    weight = column_of(weight_row)
    tiles = last // C
    for j in range(days):
        for t in range(tiles):
            at = (j * tiles + t) * K
            out_ref[:, at : at + K] = pieces_ref[j, t * C : (t + 1) * C, 0, :] / weight


def on_device(fields, eof_basis, seed_days, *, grids, days):
    rows, points = fields.shape
    f32 = jnp.float32
    own = rows // grids

    def exchange(value, axis):
        return lax.all_to_all(value, axis, 0, 0)

    pieces, held = project(fields, eof_basis, grids)
    pieces = exchange(pieces, "grid")
    shape = jax.ShapeDtypeStruct((grids, own, 1, K), f32)
    pieces = exchange(call(own_rows_kernel, shape, pieces, name="own_rows"), "grid")

    flipped, seeds = call(
        seeds_kernel,
        [
            jax.ShapeDtypeStruct((K, rows), f32),
            jax.ShapeDtypeStruct((days, C, K), f32),
        ],
        seed_days[None, :],
        pieces,
        name="seeds",
    )
    seeds = exchange(seeds, "day")
    shape = jax.ShapeDtypeStruct((days, C + 1, 1, K), f32)
    terms = exchange(call(first_kernel, shape, seeds, flipped, name="first"), "day")
    for sweep in range(1, ITERS):
        terms = call(sweep_kernel, shape, terms, flipped, name="sweep")
        terms = exchange(terms, "day")

    shapes = [
        jax.ShapeDtypeStruct((C, rows), f32),
        jax.ShapeDtypeStruct((C, K), f32),
        jax.ShapeDtypeStruct((1, K), f32),
        jax.ShapeDtypeStruct((days, C, points // days), f32),
    ]
    member, centers, weight_row, weighted = call(
        weigh_kernel, shapes, terms, flipped, held.reshape(rows, points), name="weigh"
    )
    pieces = exchange(weighted, "day")
    tiles = points // days // K
    shape = jax.ShapeDtypeStruct((days, tiles * C + 1, 1, K), f32)
    pieces = call(own_points_kernel, shape, pieces, weight_row, name="own_points")
    pieces = exchange(pieces, "day")
    shape = jax.ShapeDtypeStruct((C, points), f32)
    composites = call(finish_kernel, shape, pieces, name="finish")
    return (member.T, centers, composites)


def solution(mesh):
    return jax.shard_map(
        functools.partial(
            on_device, grids=mesh.shape["grid"], days=mesh.shape["day"]
        ),
        mesh=mesh,
        in_specs=(P("day", "grid"), P("grid", None), P()),
        out_specs=(P("day", None), P(), P(None, "grid")),
        check_vma=False,
    )
```

```python
import functools

import jax
import jax.numpy as jnp
from jax import lax
from jax.experimental import pallas as pl
from jax.experimental.pallas import tpu as pltpu
from jax.sharding import PartitionSpec as P

ITERS = 3
K = 128
C = 16
BLOCKS = 3
PARTS = 4
HIGHEST = lax.Precision.HIGHEST


def call(kernel, out_shape, *args, name, cost=None):
    flops, moved = cost or (1000000, 500000)
    return pl.pallas_call(
        kernel,
        out_shape=out_shape,
        name=name,
        compiler_params=pltpu.CompilerParams(vmem_limit_bytes=8 << 20),
        cost_estimate=pl.CostEstimate(
            flops=flops, bytes_accessed=moved, transcendentals=0
        ),
    )(*args)


def row_of(column):
    lane = lax.broadcasted_iota(jnp.int32, (C, K), 1)
    sub = lax.broadcasted_iota(jnp.int32, (C, K), 0)
    return jnp.sum(jnp.where(lane == sub, column, 0.0), axis=0, keepdims=True)


def column_of(row):
    lane = lax.broadcasted_iota(jnp.int32, (C, K), 1)
    sub = lax.broadcasted_iota(jnp.int32, (C, K), 0)
    return jnp.sum(jnp.where(lane == sub, row, 0.0), axis=1, keepdims=True)


def member_rows(flipped, centers_flipped):
    sums = []
    for c in range(C):
        offset = flipped - centers_flipped[:, c : c + 1]
        sums.append(jnp.sum(offset * offset, axis=0, keepdims=True))
    mean_square = jnp.concatenate(sums, axis=0) / K + 1e-05
    weights = 1.0 / mean_square
    return weights / jnp.sum(weights, axis=0, keepdims=True)


def total_of(ref):
    total = ref[0]
    for i in range(1, ref.shape[0]):
        total = total + ref[i]
    return total


def centers_from(terms_ref):
    total = total_of(terms_ref)
    return total[:C, 0] / column_of(total[C])


def project_kernel(
    fields_ref, basis_ref, out_ref, chunks_ref, basis_chunks_ref, sem_ref, basis_sem_ref
):
    blocks, rows = chunks_ref.shape[:2]
    parts, step = basis_chunks_ref.shape[:2]
    basis_loads = [
        pltpu.make_async_copy(
            basis_ref.at[pl.ds(j * step, step)],
            basis_chunks_ref.at[j],
            basis_sem_ref.at[j],
        )
        for j in range(parts)
    ]
    loads = [
        pltpu.make_async_copy(
            fields_ref.at[pl.ds(i * rows, rows)], chunks_ref.at[i], sem_ref.at[i]
        )
        for i in range(blocks)
    ]
    for load in basis_loads + loads:
        load.start()
    for load in basis_loads:
        load.wait()
    grids = out_ref.shape[0]
    for i in range(blocks):
        loads[i].wait()
        total = None
        for j in range(parts):
            part = jnp.dot(
                chunks_ref[i, :, j * step : (j + 1) * step],
                basis_chunks_ref[j],
                preferred_element_type=jnp.float32,
            )
            total = part if total is None else total + part
        each = rows // grids
        for r in range(each):
            out_ref[:, i * each + r, 0, :] = total[r * grids : (r + 1) * grids]


def project(fields, basis, grids):
    rows, points = fields.shape
    fields = pltpu.with_memory_space_constraint(fields, pltpu.HBM)
    basis = pltpu.with_memory_space_constraint(basis, pltpu.HBM)
    return pl.pallas_call(
        project_kernel,
        in_specs=[pl.BlockSpec(memory_space=pltpu.HBM)] * 2,
        out_specs=[pl.BlockSpec(memory_space=pltpu.VMEM)] * 2,
        out_shape=[
            jax.ShapeDtypeStruct((grids, rows // grids, 1, K), jnp.float32),
            jax.ShapeDtypeStruct((BLOCKS, rows // BLOCKS, points), jnp.bfloat16),
        ],
        scratch_shapes=[
            pltpu.VMEM((PARTS, points // PARTS, K), jnp.bfloat16),
            pltpu.SemaphoreType.DMA((BLOCKS,)),
            pltpu.SemaphoreType.DMA((PARTS,)),
        ],
        name="project",
        cost_estimate=pl.CostEstimate(
            flops=2 * rows * points * K,
            bytes_accessed=2 * points * (rows + K) + 4 * rows * K,
            transcendentals=0,
        ),
        compiler_params=pltpu.CompilerParams(vmem_limit_bytes=16 << 20),
    )(fields, basis)


def own_rows_kernel(pieces_ref, out_ref):
    total = total_of(pieces_ref)
    out_ref[...] = jnp.broadcast_to(total[None], out_ref.shape)


def seeds_kernel(days_ref, pieces_ref, flipped_ref, seeds_ref):
    own = pieces_ref.shape[1]
    amplitudes = jnp.concatenate([pieces_ref[:, r, 0, :] for r in range(own)], axis=0)
    rows = amplitudes.shape[0]
    first = lax.axis_index("day") * rows
    position = first + lax.broadcasted_iota(jnp.int32, (1, rows), 1)
    lane = lax.broadcasted_iota(jnp.int32, (C, C), 1)
    sub = lax.broadcasted_iota(jnp.int32, (C, C), 0)
    days = jnp.where(lane == sub, days_ref[...].astype(jnp.float32), 0.0)
    wanted = jnp.sum(days, axis=1, keepdims=True)
    selector = (position.astype(jnp.float32) == wanted).astype(jnp.float32)
    seeds = jnp.dot(
        selector, amplitudes, precision=HIGHEST, preferred_element_type=jnp.float32
    )
    flipped_ref[...] = amplitudes.T
    seeds_ref[...] = jnp.broadcast_to(seeds[None], seeds_ref.shape)


def store_terms(flipped, centers, out_ref):
    member = member_rows(flipped, centers.T)
    squared = member * member
    numerator = lax.dot_general(
        squared,
        flipped,
        (((1,), (1,)), ((), ())),
        precision=HIGHEST,
        preferred_element_type=jnp.float32,
    )
    weight_row = row_of(jnp.sum(squared, axis=1, keepdims=True))
    out_ref[:C, :] = numerator
    out_ref[C : C + 1, :] = weight_row


def first_kernel(seeds_ref, flipped_ref, out_ref):
    store_terms(flipped_ref[...], total_of(seeds_ref), out_ref)


def sweep_kernel(terms_ref, flipped_ref, out_ref):
    store_terms(flipped_ref[...], centers_from(terms_ref), out_ref)


def weigh_kernel(
    terms_ref, flipped_ref, fields_ref, member_ref, centers_ref, row_ref, out_ref
):
    centers = centers_from(terms_ref)
    centers_ref[...] = centers
    member = member_rows(flipped_ref[...], centers.T)
    member_ref[...] = member
    squares = member * member
    row_ref[...] = row_of(jnp.sum(squares, axis=1, keepdims=True))
    weights_bf = squares.astype(jnp.bfloat16)
    days, _, width = out_ref.shape
    for j in range(days):
        out_ref[j] = jnp.dot(
            weights_bf,
            fields_ref[:, j * width : (j + 1) * width],
            preferred_element_type=jnp.float32,
        )


def own_points_kernel(pieces_ref, row_ref, out_ref):
    total = total_of(pieces_ref)
    tiles = total.shape[1] // K
    for i in range(out_ref.shape[0]):
        for t in range(tiles):
            out_ref[i, t * C : (t + 1) * C, 0, :] = total[:, t * K : (t + 1) * K]
        out_ref[i, tiles * C, :, :] = row_ref[...]


def finish_kernel(pieces_ref, out_ref):
    days, last = pieces_ref.shape[0], pieces_ref.shape[1] - 1
    weight_row = pieces_ref[0, last]
    for j in range(1, days):
        weight_row = weight_row + pieces_ref[j, last]
    weight = column_of(weight_row)
    tiles = last // C
    for j in range(days):
        for t in range(tiles):
            at = (j * tiles + t) * K
            out_ref[:, at : at + K] = pieces_ref[j, t * C : (t + 1) * C, 0, :] / weight


def on_device(fields, eof_basis, seed_days, *, grids, days):
    rows, points = fields.shape
    f32 = jnp.float32
    own = rows // grids

    def exchange(value, axis):
        return lax.all_to_all(value, axis, 0, 0)

    pieces, held = project(fields, eof_basis, grids)
    pieces = exchange(pieces, "grid")
    shape = jax.ShapeDtypeStruct((grids, own, 1, K), f32)
    pieces = exchange(call(own_rows_kernel, shape, pieces, name="own_rows"), "grid")

    flipped, seeds = call(
        seeds_kernel,
        [
            jax.ShapeDtypeStruct((K, rows), f32),
            jax.ShapeDtypeStruct((days, C, K), f32),
        ],
        seed_days[None, :],
        pieces,
        name="seeds",
    )
    seeds = exchange(seeds, "day")
    shape = jax.ShapeDtypeStruct((C + 1, K), f32)

    def spread(terms):
        copies = jnp.broadcast_to(terms[None, :, None, :], (days, C + 1, 1, K))
        return exchange(copies, "day")

    terms = spread(call(first_kernel, shape, seeds, flipped, name="first"))
    for sweep in range(1, ITERS):
        terms = spread(call(sweep_kernel, shape, terms, flipped, name="sweep"))

    shapes = [
        jax.ShapeDtypeStruct((C, rows), f32),
        jax.ShapeDtypeStruct((C, K), f32),
        jax.ShapeDtypeStruct((1, K), f32),
        jax.ShapeDtypeStruct((days, C, points // days), f32),
    ]
    member, centers, weight_row, weighted = call(
        weigh_kernel, shapes, terms, flipped, held.reshape(rows, points), name="weigh"
    )
    pieces = exchange(weighted, "day")
    tiles = points // days // K
    shape = jax.ShapeDtypeStruct((days, tiles * C + 1, 1, K), f32)
    pieces = call(own_points_kernel, shape, pieces, weight_row, name="own_points")
    pieces = exchange(pieces, "day")
    shape = jax.ShapeDtypeStruct((C, points), f32)
    composites = call(finish_kernel, shape, pieces, name="finish")
    return (member.T, centers, composites)


def solution(mesh):
    return jax.shard_map(
        functools.partial(
            on_device, grids=mesh.shape["grid"], days=mesh.shape["day"]
        ),
        mesh=mesh,
        in_specs=(P("day", "grid"), P("grid", None), P()),
        out_specs=(P("day", None), P(), P(None, "grid")),
        check_vma=False,
    )
```
